32 devices in a mesh: row: 4 (over y, core), col: 8 (over z, x).
Axes of the slice: x: 2, y: 2, z: 4, core: 2. Of those that a mesh axis runs over, the one named last changes fastest.
Arguments:
- transfer: bfloat16 [2048, 2, 512, 256], P(('row', 'col')), may hold values from -0.65625 to 0.65625
- target: bfloat16 [2048, 2, 32, 512], P(('row', 'col')), may hold values from -6 to 6
- zone_mask: int32 [32, 512], replicated, may hold values 0 or 1
- dark_weight: float32 [32], replicated, may hold values from 1 to 4
- reg_weight: float32 [2048], P(('row', 'col')), may hold values from 0.05 to 2
- momentum: float32 [1], replicated, may hold values from 0.2 to 0.8
Outputs:
- filters: float32 [32, 256, 1024], P(None, ('row', 'col'))
- residual: float32 [32, 256, 1024], P(None, ('row', 'col'))
The draws below stay inside these ranges and needn't reach their ends.
All inputs are finite; a program needn't handle non-finite values.
Results may differ from the reference program's by a relative error of at most 0.0059.
Values may be sent and summed in bfloat16 or wider, within the bound.
No kernel may reach another device: no remote copies, remote signals or barrier semaphores. Data moves between devices by JAX's collectives and lax.ppermute only.
A program may use at most 128 MiB of HBM per device.

```python
import math
import jax
import jax.numpy as jnp
from jax import lax

L = 256
M = 512
K = 1024
F = 2048
TARGETS = 32
ITERS = 2


def draw_transfer(key, part):
    base_key, row_key, col_key = jax.random.split(key, 3)
    base = jax.random.truncated_normal(base_key, -4.0, 4.0, (F, 2, M, L), jnp.float32)
    row_scale = 3.0 ** (jax.random.uniform(row_key, (M,), jnp.float32) - 0.5)
    col_scale = 3.0 ** (jnp.arange(L, dtype=jnp.float32) / max(L - 1, 1) + jax.random.uniform(col_key, (L,), jnp.float32))
    scaled = base * row_scale[:, None] * col_scale[None, :] / (3.0 * math.sqrt(2.0 * M))
    return scaled.astype(jnp.bfloat16)


def touch_ends(values, stream_key, smallest, top_value):
    dims = values.shape
    spot = [jax.random.randint(jax.random.fold_in(stream_key, axis), (), 0, dims[axis]) for axis in range(len(dims))]
    values = values.at[tuple(spot)].set(smallest)
    longest = dims.index(max(dims))
    spot[longest] = (spot[longest] + 1) % dims[longest]
    return values.at[tuple(spot)].set(top_value)


def levels(own_key, dims, pieces, smallest, top_value):
    loudness = 1.0
    for dim, shards_of in pieces:
        heights = jax.random.uniform(jax.random.fold_in(jax.random.fold_in(own_key, 6), dim), (shards_of,), jnp.float32, smallest / len(pieces), top_value / len(pieces))
        loudness = loudness * jnp.repeat(jnp.exp(heights), dims[dim] // shards_of).reshape((-1,) + (1,) * (len(dims) - 1 - dim))
    return loudness


def gaussian(rng, dims, deviation, bound, shards=(), held_as=jnp.bfloat16):
    drawn = deviation * jax.random.normal(rng, dims, jnp.float32)
    if shards:
        drawn = drawn * levels(rng, dims, shards, -0.22, 0.18)
    return jnp.clip(drawn, -bound, bound).astype(held_as)


def setup_inputs(seed: int = 0) -> dict:
    keys = jax.random.split(jax.random.key(seed), 7)
    transfer = draw_transfer(jax.random.fold_in(keys[6], 71), 0)
    target = gaussian(keys[1], (F, 2, TARGETS, M), 1.0, 6.0, ((0, 32),))
    zone_mask = touch_ends((jax.random.randint(keys[2], (TARGETS, M), 0, 2) < 1).astype(jnp.int32), jax.random.fold_in(keys[2], 1), 0, 1)
    dark_weight = jnp.clip(jnp.exp(jax.random.uniform(keys[3], (TARGETS,), jnp.float32, math.log(1.0), math.log(4.0))), 1.0, 4.0)
    reg_weight = jnp.clip(jnp.exp(math.log(2.0) - 3.6888794 * jax.random.uniform(keys[4], (F,), jnp.float32) ** levels(keys[4], (F,), ((0, 32),), -0.2, 0.2)), 0.05, 2.0)
    momentum = jnp.clip(jax.random.uniform(keys[5], (ITERS - 1,), jnp.float32, 0.2, 0.8), 0.2, 0.8)
    return dict(transfer=transfer, target=target, zone_mask=zone_mask, dark_weight=dark_weight, reg_weight=reg_weight, momentum=momentum)


def build_table(taps, bins):
    tap_index = jnp.arange(taps, dtype=jnp.int32)[:, None]
    bin_index = jnp.arange(bins, dtype=jnp.int32)[None, :]
    phase = (tap_index * bin_index % bins).astype(jnp.float32) * (2.0 * math.pi / bins)
    return jnp.stack([jnp.cos(phase), -jnp.sin(phase)], axis=1) / math.sqrt(bins)

def reference(transfer, target, zone_mask, dark_weight, reg_weight, momentum):
    dft_table = build_table(K, F)
    mic_gains = jnp.where(zone_mask == 1, jnp.ones_like(dark_weight)[:, None], dark_weight[:, None])
    count = F // 64
    transfer_blocks = transfer.reshape(count, 64, 2, M, L)
    reg_term = reg_weight[:, None, None, None]

    def back_block(operands):
        response = operands[0].astype(jnp.float32)
        errors = operands[1].astype(jnp.float32)
        back_real = jnp.einsum('fml,ftm->ftl', response[:, 0], errors[:, 0]) + jnp.einsum('fml,ftm->ftl', response[:, 1], errors[:, 1])
        back_imag = jnp.einsum('fml,ftm->ftl', response[:, 0], errors[:, 1]) - jnp.einsum('fml,ftm->ftl', response[:, 1], errors[:, 0])
        return jnp.stack([back_real, back_imag], axis=1)

    def normal_block(operands):
        response = operands[0].astype(jnp.float32)
        spectrum = operands[1].astype(jnp.float32)
        press_real = jnp.einsum('fml,ftl->ftm', response[:, 0], spectrum[:, 0]) - jnp.einsum('fml,ftl->ftm', response[:, 1], spectrum[:, 1])
        press_imag = jnp.einsum('fml,ftl->ftm', response[:, 0], spectrum[:, 1]) + jnp.einsum('fml,ftl->ftm', response[:, 1], spectrum[:, 0])
        err_real = lax.optimization_barrier((mic_gains * press_real).astype(jnp.bfloat16)).astype(jnp.float32)
        err_imag = lax.optimization_barrier((mic_gains * press_imag).astype(jnp.bfloat16)).astype(jnp.float32)
        back_real = jnp.einsum('fml,ftm->ftl', response[:, 0], err_real) + jnp.einsum('fml,ftm->ftl', response[:, 1], err_imag)
        back_imag = jnp.einsum('fml,ftm->ftl', response[:, 0], err_imag) - jnp.einsum('fml,ftm->ftl', response[:, 1], err_real)
        return jnp.stack([back_real, back_imag], axis=1)

    def to_taps(spectrum):
        return jnp.einsum('fctl,kcf->tlk', spectrum, dft_table, precision=lax.Precision.HIGHEST)

    def operator(direction):
        spectrum = jnp.einsum('tlk,kcf->fctl', direction, dft_table, precision=lax.Precision.HIGHEST).astype(jnp.bfloat16)
        back = lax.map(normal_block, (transfer_blocks, spectrum.reshape(count, 64, 2, TARGETS, L)))
        back = back.reshape(F, 2, TARGETS, L)
        return to_taps(back + reg_term * spectrum.astype(jnp.float32))
    rhs_error = jnp.where(zone_mask[None, None] == 1, target, jnp.zeros_like(target))
    rhs_back = lax.map(back_block, (transfer_blocks, rhs_error.reshape(count, 64, 2, TARGETS, M)))
    rhs = to_taps(rhs_back.reshape(F, 2, TARGETS, L))
    filters = jnp.zeros_like(rhs)
    residual = rhs
    direction = rhs
    for iteration in range(ITERS):
        image_taps = operator(direction)
        along_sum = jnp.sum(residual * direction)
        bend_sum = jnp.sum(direction * image_taps)
        step_size = along_sum / bend_sum
        filters = filters + step_size * direction
        residual = residual - step_size * image_taps
        if iteration + 1 < ITERS:
            direction = residual + momentum[iteration] * direction
    return (filters, residual)
```

```python
import math

import jax
import jax.numpy as jnp
from jax import lax
from jax.experimental import pallas as pl
from jax.experimental.pallas import tpu as pltpu
from jax.sharding import PartitionSpec as P

K = 1024
F = 2048
ITERS = 2
AXES = ("row", "col")
BF16 = jnp.bfloat16
F32 = jnp.float32
NT = (((1,), (1,)), ((), ()))
VMEM_BYTES = 60 * 2**20


def dot_nn(a, b):
    return jnp.dot(a, b, preferred_element_type=F32)


def dot_nt(a, b):
    return lax.dot_general(a, b, NT, preferred_element_type=F32)


def build_table(taps, bins):
    tap_index = jnp.arange(taps, dtype=jnp.int32)[:, None]
    bin_index = jnp.arange(bins, dtype=jnp.int32)[None, :]
    phase = (tap_index * bin_index % bins).astype(jnp.float32) * (2.0 * math.pi / bins)
    return jnp.stack([jnp.cos(phase), -jnp.sin(phase)], axis=1) / math.sqrt(bins)


def plain_body(transfer, target, zone_mask, dark_weight, reg_weight, momentum):
    dft_table = build_table(K, F)
    mic_gains = jnp.where(zone_mask == 1, jnp.float32(1.0), dark_weight[:, None])
    weight_real = transfer[:, 0]
    weight_imag = transfer[:, 1]
    reg_term = reg_weight[:, None, None]

    def to_taps(spectrum):
        regrouped = lax.all_to_all(spectrum, AXES, split_axis=3, concat_axis=0, tiled=True)
        return jnp.einsum("fctl,kcf->tlk", regrouped, dft_table, precision=lax.Precision.HIGHEST)

    def contract(spec, first, second):
        return jnp.einsum(spec, first, second, preferred_element_type=jnp.float32)

    def back_project(err_real, err_imag):
        spec = "fml,ftm->ftl"
        back_real = contract(spec, weight_real, err_real) + contract(spec, weight_imag, err_imag)
        back_imag = contract(spec, weight_real, err_imag) - contract(spec, weight_imag, err_real)
        return back_real, back_imag

    rhs_error = jnp.where(zone_mask[None, None] == 1, target, jnp.zeros_like(target))
    rhs = to_taps(jnp.stack(back_project(rhs_error[:, 0], rhs_error[:, 1]), axis=1))
    filters = jnp.zeros_like(rhs)
    residual = rhs
    direction = rhs
    for iteration in range(ITERS):
        along_term = jnp.sum(residual * direction)
        to_spectrum = jnp.einsum(
            "tlk,kcf->fctl", direction, dft_table, precision=lax.Precision.HIGHEST
        ).astype(jnp.bfloat16)
        spec = lax.all_to_all(to_spectrum, AXES, split_axis=0, concat_axis=3, tiled=True)
        spec_real = spec[:, 0]
        spec_imag = spec[:, 1]
        form = "fml,ftl->ftm"
        press_real = contract(form, weight_real, spec_real) - contract(form, weight_imag, spec_imag)
        press_imag = contract(form, weight_real, spec_imag) + contract(form, weight_imag, spec_real)
        back_real, back_imag = back_project(
            (mic_gains * press_real).astype(jnp.bfloat16),
            (mic_gains * press_imag).astype(jnp.bfloat16),
        )
        image_taps = to_taps(
            jnp.stack(
                [
                    back_real + reg_term * spec_real.astype(jnp.float32),
                    back_imag + reg_term * spec_imag.astype(jnp.float32),
                ],
                axis=1,
            )
        )
        along_sum, bend_sum = lax.psum((along_term, jnp.sum(direction * image_taps)), AXES)
        step_size = along_sum / bend_sum
        filters = filters + step_size * direction
        residual = residual - step_size * image_taps
        if iteration + 1 < ITERS:
            direction = residual + momentum[iteration] * direction
    return (filters, residual)


def split_table(devices, bins, taps):
    local = bins // devices
    tap = jnp.arange(taps, dtype=jnp.int32)
    scale = 2.0 * math.pi / bins
    coarse = (jnp.arange(devices, dtype=jnp.int32)[:, None] * local * tap[None, :]) % bins
    fine = (jnp.arange(local, dtype=jnp.int32)[:, None] * tap[None, :]) % bins
    coarse = coarse.astype(F32) * scale
    fine = fine.astype(F32) * scale
    norm = 1.0 / math.sqrt(bins)
    cos_c, sin_c = (jnp.cos(coarse) * norm)[:, None], (jnp.sin(coarse) * norm)[:, None]
    cos_f, sin_f = jnp.cos(fine)[None], jnp.sin(fine)[None]
    cos_c, sin_c, cos_f, sin_f = lax.optimization_barrier((cos_c, sin_c, cos_f, sin_f))
    table = jnp.stack([cos_c * cos_f - sin_c * sin_f, -(sin_c * cos_f + cos_c * sin_f)], axis=1)
    high = lax.reduce_precision(table, 8, 7)
    shape = (2 * bins, taps)
    return high.astype(BF16).reshape(shape), (table - high).astype(BF16).reshape(shape)


LANES = 128


def turn_out(turn_ref, out_ref, targets):
    devices, _, width = out_ref.shape
    step_rows = targets * width
    blocks = turn_ref.shape[0] // step_rows
    each = devices // blocks

    def step(pair, carry):
        for block in range(blocks):
            halves = []
            for side in range(2):
                start = block * step_rows + (2 * pair + side) * width
                halves.append(turn_ref[pl.ds(start, width), :].T.reshape(each, 8, width))
            both = jnp.concatenate(halves, axis=1).astype(BF16)
            out_ref[block * each : (block + 1) * each, pl.ds(16 * pair, 16), :] = both
        return carry

    lax.fori_loop(0, targets // 2, step, 0)


def turn_in(in_ref, turn_ref, targets):
    devices, _, width = in_ref.shape
    step_rows = targets * width
    blocks = turn_ref.shape[0] // step_rows
    each = devices // blocks

    def step(pair, carry):
        for block in range(blocks):
            part = in_ref[block * each : (block + 1) * each, pl.ds(16 * pair, 16), :].astype(F32)
            for side in range(2):
                half = part[:, 8 * side : 8 * side + 8, :].reshape(LANES, width)
                start = block * step_rows + (2 * pair + side) * width
                turn_ref[pl.ds(start, width), :] = half.T
        return carry

    lax.fori_loop(0, targets // 2, step, 0)


def load_bin(turn_ref, row, targets, stride):
    step_rows = targets * stride
    return jnp.concatenate(
        [
            turn_ref[pl.ds(block * step_rows + row, targets, stride=stride), :]
            for block in range(turn_ref.shape[0] // step_rows)
        ],
        axis=1,
    )


def store_bin(turn_ref, row, targets, stride, values):
    step_rows = targets * stride
    for block in range(turn_ref.shape[0] // step_rows):
        part = values[:, block * LANES : (block + 1) * LANES]
        turn_ref[pl.ds(block * step_rows + row, targets, stride=stride), :] = part


def store_sums(out_ref, along, bend):
    row = lax.broadcasted_iota(jnp.int32, along.shape, 0)
    value = jnp.where(row < 3, along, bend)
    first = value.astype(BF16).astype(F32)
    second = (value - first).astype(BF16).astype(F32)
    third = value - first - second
    term = jnp.where(row % 3 == 0, first, jnp.where(row % 3 == 1, second, third))
    term = jnp.where(row < 6, term, 0.0).astype(BF16)
    rows = out_ref.shape[1]
    out_ref[:, rows - 8 : rows, :] = jnp.broadcast_to(term[None], (out_ref.shape[0],) + term.shape)


def step_of(back_ref):
    rows = back_ref.shape[1]
    sums = jnp.sum(back_ref[:, rows - 8 : rows, :].astype(F32), axis=0)
    along = sums[0:1, 0:1] + sums[1:2, 0:1] + sums[2:3, 0:1]
    bend = sums[3:4, 0:1] + sums[4:5, 0:1] + sums[5:6, 0:1]
    return along / bend


def back_of(err, weight, half):
    turned = jnp.concatenate([err[half:], -err[:half]], axis=0)
    return dot_nn(err, weight[0]) + dot_nn(turned, weight[1])


GROUP = 8


def start_weights(w_hbm, w_buf, sems):
    groups = w_buf.shape[0] // GROUP
    copies = [
        pltpu.make_async_copy(
            w_hbm.at[pl.ds(g * GROUP, GROUP)], w_buf.at[pl.ds(g * GROUP, GROUP)], sems.at[g]
        )
        for g in range(groups)
    ]
    for copy in copies:
        copy.start()


def wait_weights(w_hbm, w_buf, sems, g):
    pltpu.make_async_copy(
        w_hbm.at[pl.ds(g * GROUP, GROUP)], w_buf.at[pl.ds(g * GROUP, GROUP)], sems.at[g]
    ).wait()


def rhs_kernel(target_ref, mask_ref, w_hbm, out_ref, w_buf, back_buf, sems):
    bins, _, targets, mics = target_ref.shape
    start_weights(w_hbm, w_buf, sems)
    bright = mask_ref[...] == 1
    bright = jnp.concatenate([bright, bright], axis=0)

    def group(g, carry):
        wait_weights(w_hbm, w_buf, sems, g)
        for b in range(GROUP):
            j = g * GROUP + b
            wanted = target_ref[j].reshape(2 * targets, mics).astype(F32)
            err = jnp.where(bright, wanted, 0.0).astype(BF16)
            back = back_of(err, w_buf.at[j], targets)
            store_bin(back_buf, j, targets, 2 * bins, back[:targets])
            store_bin(back_buf, bins + j, targets, 2 * bins, back[targets:])
        return carry

    lax.fori_loop(0, bins // GROUP, group, 0)
    turn_out(back_buf, out_ref, targets)


def normal_kernel(
    spec_ref, mask_ref, dark_ref, reg_ref, along_ref, w_hbm,
    out_ref, w_buf, spec_buf, back_buf, sems,
):
    bins = w_buf.shape[0]
    targets = mask_ref.shape[0]
    start_weights(w_hbm, w_buf, sems)
    gains = jnp.where(mask_ref[...] == 1, jnp.float32(1.0), dark_ref[...])
    gains = jnp.concatenate([gains, gains], axis=0)
    turn_in(spec_ref, spec_buf, targets)

    def group(g, bend):
        wait_weights(w_hbm, w_buf, sems, g)
        for b in range(GROUP):
            j = g * GROUP + b
            weight = w_buf.at[j]
            real = load_bin(spec_buf, j, targets, 2 * bins)
            imag = load_bin(spec_buf, bins + j, targets, 2 * bins)
            wide = jnp.concatenate([real, imag], axis=0)
            spec = wide.astype(BF16)
            turned = jnp.concatenate([-imag, real], axis=0).astype(BF16)
            press = dot_nt(spec, weight[0]) + dot_nt(turned, weight[1])
            back = back_of((gains * press).astype(BF16), weight, targets)
            back = back + reg_ref[j] * wide
            bend = bend + wide * back
            store_bin(back_buf, j, targets, 2 * bins, back[:targets])
            store_bin(back_buf, bins + j, targets, 2 * bins, back[targets:])
        return bend

    bend = lax.fori_loop(0, bins // GROUP, group, jnp.zeros((2 * targets, w_buf.shape[3]), F32))
    turn_out(back_buf, out_ref, targets)
    store_sums(out_ref, along_ref[...], jnp.sum(bend))


CHUNK = 8


def start_table(high_hbm, low_hbm, high_buf, low_buf, sems):
    rows = high_buf.shape[0] // 4
    for c in range(4):
        part = pl.ds(c * rows, rows)
        pltpu.make_async_copy(high_hbm.at[part], high_buf.at[part], sems.at[0, c]).start()
        pltpu.make_async_copy(low_hbm.at[part], low_buf.at[part], sems.at[1, c]).start()


def taps_of(back_ref, count, high_hbm, low_hbm, high_buf, low_buf, sems):
    rows = high_buf.shape[0] // 4
    per = back_ref.shape[0] // 4
    total = None
    for c in range(4):
        part = pl.ds(c * rows, rows)
        pltpu.make_async_copy(high_hbm.at[part], high_buf.at[part], sems.at[0, c]).wait()
        pltpu.make_async_copy(low_hbm.at[part], low_buf.at[part], sems.at[1, c]).wait()
        block = jnp.concatenate([back_ref[c * per + d, :count, :] for d in range(per)], axis=1)
        term = dot_nn(block, high_buf[part, :]) + dot_nn(block, low_buf[part, :])
        total = term if total is None else total + term
    return total


def spectrum_to(out_ref, direction, high_buf, low_buf):
    rows = high_buf.shape[0] // 4
    per = out_ref.shape[0] // 4
    width = out_ref.shape[2]
    count = direction.shape[0]
    high = direction.astype(BF16)
    low = (direction - high.astype(F32)).astype(BF16)
    both = jnp.concatenate([high, low], axis=0)
    for c in range(4):
        part = pl.ds(c * rows, rows)
        wide = dot_nt(both, high_buf[part, :])
        spec = wide[:count] + wide[count:] + dot_nt(high, low_buf[part, :])
        for d in range(per):
            out_ref[c * per + d] = spec[:, d * width : (d + 1) * width].astype(BF16)


def first_kernel(
    back_ref, high_hbm, low_hbm, rhs_ref, spec_ref, along_ref, high_buf, low_buf, sems
):
    start_table(high_hbm, low_hbm, high_buf, low_buf, sems)
    rhs = taps_of(back_ref, rhs_ref.shape[0], high_hbm, low_hbm, high_buf, low_buf, sems)
    rhs_ref[...] = rhs
    along_ref[...] = jnp.broadcast_to(jnp.sum(rhs * rhs), along_ref.shape)
    spectrum_to(spec_ref, rhs, high_buf, low_buf)


def middle_kernel(
    back_ref, rhs_ref, momentum_ref, high_hbm, low_hbm,
    filters_ref, residual_ref, direction_ref, spec_ref, along_ref, high_buf, low_buf, sems,
):
    start_table(high_hbm, low_hbm, high_buf, low_buf, sems)
    step = step_of(back_ref)
    image = taps_of(back_ref, residual_ref.shape[0], high_hbm, low_hbm, high_buf, low_buf, sems)
    rhs = rhs_ref[...]
    residual = rhs - step * image
    direction = residual + momentum_ref[0] * rhs
    filters_ref[...] = step * rhs
    residual_ref[...] = residual
    direction_ref[...] = direction
    along_ref[...] = jnp.broadcast_to(jnp.sum(residual * direction), along_ref.shape)
    spectrum_to(spec_ref, direction, high_buf, low_buf)


def last_kernel(
    back_ref, filters_ref, residual_ref, direction_ref, high_hbm, low_hbm,
    filters_out, residual_out, high_buf, low_buf, sems,
):
    start_table(high_hbm, low_hbm, high_buf, low_buf, sems)
    step = step_of(back_ref)
    image = taps_of(back_ref, residual_ref.shape[0], high_hbm, low_hbm, high_buf, low_buf, sems)
    filters_out[...] = filters_ref[...] + step * direction_ref[...]
    residual_out[...] = residual_ref[...] - step * image


def vmem():
    return pl.BlockSpec(memory_space=pltpu.VMEM)


def smem():
    return pl.BlockSpec(memory_space=pltpu.SMEM)


def hbm():
    return pl.BlockSpec(memory_space=pl.ANY)


def kernel_body(transfer, target, zone_mask, dark_weight, reg_weight, momentum):
    bins, _, mics, speakers = transfer.shape
    targets = target.shape[2]
    devices = F // bins
    rows = targets * (speakers // devices)
    block = jax.ShapeDtypeStruct((devices, rows, 2 * bins), BF16)
    summed = jax.ShapeDtypeStruct((devices, rows + 8, 2 * bins), BF16)
    tile = jax.ShapeDtypeStruct((8, 128), F32)
    taps = jax.ShapeDtypeStruct((rows, K), F32)
    params = pltpu.CompilerParams(vmem_limit_bytes=VMEM_BYTES)
    high, low = split_table(devices, F, K)
    dark = dark_weight[:, None]
    bin_scratch = [
        pltpu.VMEM((speakers // LANES * targets * 2 * bins, LANES), F32),
        pltpu.SemaphoreType.DMA((bins // GROUP,)),
    ]
    weights = pltpu.VMEM(transfer.shape, BF16)
    table_scratch = [
        pltpu.VMEM(high.shape, BF16),
        pltpu.VMEM(low.shape, BF16),
        pltpu.SemaphoreType.DMA((2, 4)),
    ]

    def exchange(payload):
        return lax.all_to_all(payload, AXES, split_axis=0, concat_axis=0, tiled=True)

    def normal(spec, along):
        return pl.pallas_call(
            normal_kernel,
            in_specs=[vmem(), vmem(), vmem(), smem(), vmem(), hbm()],
            out_specs=vmem(),
            out_shape=summed,
            scratch_shapes=[weights, bin_scratch[0]] + bin_scratch,
            compiler_params=params,
            name="normal",
        )(spec, zone_mask, dark, reg_weight, along, transfer)

    back = pl.pallas_call(
        rhs_kernel,
        in_specs=[vmem(), vmem(), hbm()],
        out_specs=vmem(),
        out_shape=block,
        scratch_shapes=[weights] + bin_scratch,
        compiler_params=params,
        name="rhs_back",
    )(target, zone_mask, transfer)
    rhs, spec, along = pl.pallas_call(
        first_kernel,
        in_specs=[vmem(), hbm(), hbm()],
        out_specs=[vmem(), vmem(), vmem()],
        out_shape=[taps, block, tile],
        scratch_shapes=table_scratch,
        compiler_params=params,
        name="first_taps",
    )(exchange(back), high, low)
    back = normal(exchange(spec), along)
    filters, residual, direction, spec, along = pl.pallas_call(
        middle_kernel,
        in_specs=[vmem(), vmem(), smem(), hbm(), hbm()],
        out_specs=[vmem()] * 5,
        out_shape=[taps, taps, taps, block, tile],
        scratch_shapes=table_scratch,
        compiler_params=params,
        name="middle_taps",
    )(exchange(back), rhs, momentum, high, low)
    back = normal(exchange(spec), along)
    filters, residual = pl.pallas_call(
        last_kernel,
        in_specs=[vmem()] * 4 + [hbm(), hbm()],
        out_specs=[vmem(), vmem()],
        out_shape=[taps, taps],
        scratch_shapes=table_scratch,
        compiler_params=params,
        name="last_taps",
    )(exchange(back), filters, residual, direction, high, low)
    shape = (targets, speakers // devices, K)
    return filters.reshape(shape), residual.reshape(shape)


def body(transfer, target, *rest):
    bins, _, mics, speakers = transfer.shape
    devices = F // bins
    whole_tiles = (
        bins == 64
        and speakers == 8 * devices
        and speakers % 128 == 0
        and mics % 128 == 0
        and target.shape[2] == 32
        and devices % 4 == 0
    )
    return (kernel_body if whole_tiles else plain_body)(transfer, target, *rest)


def solution(mesh):
    in_specs = (
        P(AXES, None, None, None),
        P(AXES, None, None, None),
        P(),
        P(),
        P(AXES),
        P(),
    )
    out_specs = (P(None, AXES, None), P(None, AXES, None))
    return jax.shard_map(body, mesh=mesh, in_specs=in_specs, out_specs=out_specs, check_vma=False)
```

```python
import math

import jax
import jax.numpy as jnp
import numpy as np
from jax import lax
from jax.experimental import pallas as pl
from jax.experimental.pallas import tpu as pltpu
from jax.sharding import PartitionSpec as P

K = 1024
F = 2048
ITERS = 2
AXES = ("row", "col")
BF16 = jnp.bfloat16
F32 = jnp.float32
NT = (((1,), (1,)), ((), ()))
VMEM_BYTES = 28 * 2**20


def dot_nn(a, b):
    return jnp.dot(a, b, preferred_element_type=F32)


def dot_nt(a, b):
    return lax.dot_general(a, b, NT, preferred_element_type=F32)


def build_table(taps, bins):
    tap_index = jnp.arange(taps, dtype=jnp.int32)[:, None]
    bin_index = jnp.arange(bins, dtype=jnp.int32)[None, :]
    phase = (tap_index * bin_index % bins).astype(jnp.float32) * (2.0 * math.pi / bins)
    return jnp.stack([jnp.cos(phase), -jnp.sin(phase)], axis=1) / math.sqrt(bins)


def plain_body(transfer, target, zone_mask, dark_weight, reg_weight, momentum):
    dft_table = build_table(K, F)
    mic_gains = jnp.where(zone_mask == 1, jnp.float32(1.0), dark_weight[:, None])
    weight_real = transfer[:, 0]
    weight_imag = transfer[:, 1]
    reg_term = reg_weight[:, None, None]

    def to_taps(spectrum):
        regrouped = lax.all_to_all(spectrum, AXES, split_axis=3, concat_axis=0, tiled=True)
        return jnp.einsum("fctl,kcf->tlk", regrouped, dft_table, precision=lax.Precision.HIGHEST)

    def contract(spec, first, second):
        return jnp.einsum(spec, first, second, preferred_element_type=jnp.float32)

    def back_project(err_real, err_imag):
        spec = "fml,ftm->ftl"
        back_real = contract(spec, weight_real, err_real) + contract(spec, weight_imag, err_imag)
        back_imag = contract(spec, weight_real, err_imag) - contract(spec, weight_imag, err_real)
        return back_real, back_imag

    rhs_error = jnp.where(zone_mask[None, None] == 1, target, jnp.zeros_like(target))
    rhs = to_taps(jnp.stack(back_project(rhs_error[:, 0], rhs_error[:, 1]), axis=1))
    filters = jnp.zeros_like(rhs)
    residual = rhs
    direction = rhs
    for iteration in range(ITERS):
        along_term = jnp.sum(residual * direction)
        to_spectrum = jnp.einsum(
            "tlk,kcf->fctl", direction, dft_table, precision=lax.Precision.HIGHEST
        ).astype(jnp.bfloat16)
        spec = lax.all_to_all(to_spectrum, AXES, split_axis=0, concat_axis=3, tiled=True)
        spec_real = spec[:, 0]
        spec_imag = spec[:, 1]
        form = "fml,ftl->ftm"
        press_real = contract(form, weight_real, spec_real) - contract(form, weight_imag, spec_imag)
        press_imag = contract(form, weight_real, spec_imag) + contract(form, weight_imag, spec_real)
        back_real, back_imag = back_project(
            (mic_gains * press_real).astype(jnp.bfloat16),
            (mic_gains * press_imag).astype(jnp.bfloat16),
        )
        image_taps = to_taps(
            jnp.stack(
                [
                    back_real + reg_term * spec_real.astype(jnp.float32),
                    back_imag + reg_term * spec_imag.astype(jnp.float32),
                ],
                axis=1,
            )
        )
        along_sum, bend_sum = lax.psum((along_term, jnp.sum(direction * image_taps)), AXES)
        step_size = along_sum / bend_sum
        filters = filters + step_size * direction
        residual = residual - step_size * image_taps
        if iteration + 1 < ITERS:
            direction = residual + momentum[iteration] * direction
    return (filters, residual)


def table_factors(devices, bins, taps):
    local = bins // devices
    tap = np.arange(taps)
    scale = 2.0 * math.pi / bins
    coarse = (np.arange(devices // 2)[:, None] * local * tap[None, :]) % bins * scale
    fine = (np.arange(local)[:, None] * tap[None, :]) % bins * scale
    norm = 1.0 / math.sqrt(bins)
    factors = (np.cos(coarse) * norm, np.sin(coarse) * norm, np.cos(fine), np.sin(fine))
    return jnp.asarray(np.concatenate(factors).astype(np.float32))


def table_rows(d, bins, factors, high_ref, low_ref):
    half = factors.shape[0] // 2 - bins
    cos_c = factors[pl.ds(d, 1), :]
    sin_c = factors[pl.ds(half + d, 1), :]
    cos_f = factors[2 * half : 2 * half + bins, :]
    sin_f = factors[2 * half + bins :, :]
    odd = lax.broadcasted_iota(jnp.int32, cos_f.shape, 1) % 2
    sign = (1 - 2 * odd).astype(BF16)
    parts = (cos_c * cos_f - sin_c * sin_f, -(sin_c * cos_f + cos_c * sin_f))
    for c, value in enumerate(parts):
        high = value.astype(BF16)
        low = (value - high.astype(F32)).astype(BF16)
        here = pl.ds((2 * d + c) * bins, bins)
        there = pl.ds((2 * (d + half) + c) * bins, bins)
        high_ref[here, :] = high
        low_ref[here, :] = low
        high_ref[there, :] = high * sign
        low_ref[there, :] = low * sign


LANES = 128
PAD = 8


def turn_out(turn_ref, out_ref, targets):
    devices, _, width = out_ref.shape
    pitch = width + PAD
    step_rows = targets * pitch
    blocks = turn_ref.shape[0] // step_rows
    each = devices // blocks

    def step(pair, carry):
        for block in range(blocks):
            halves = []
            for side in range(2):
                start = block * step_rows + (2 * pair + side) * pitch
                halves.append(turn_ref[pl.ds(start, width), :].T.reshape(each, 8, width))
            both = jnp.concatenate(halves, axis=1).astype(BF16)
            out_ref[block * each : (block + 1) * each, pl.ds(16 * pair, 16), :] = both
        return carry

    lax.fori_loop(0, targets // 2, step, 0)


def turn_in(in_ref, turn_ref, targets):
    devices, _, width = in_ref.shape
    pitch = width + PAD
    step_rows = targets * pitch
    blocks = turn_ref.shape[0] // step_rows
    each = devices // blocks

    def step(pair, carry):
        for block in range(blocks):
            part = in_ref[block * each : (block + 1) * each, pl.ds(16 * pair, 16), :].astype(F32)
            for side in range(2):
                half = part[:, 8 * side : 8 * side + 8, :].reshape(LANES, width)
                start = block * step_rows + (2 * pair + side) * pitch
                turn_ref[pl.ds(start, width), :] = half.T
        return carry

    lax.fori_loop(0, targets // 2, step, 0)


def load_bin(turn_ref, row, targets, width):
    stride = width + PAD
    step_rows = targets * stride
    return jnp.concatenate(
        [
            turn_ref[pl.ds(block * step_rows + row, targets, stride=stride), :]
            for block in range(turn_ref.shape[0] // step_rows)
        ],
        axis=1,
    )


def store_bin(turn_ref, row, targets, width, values):
    stride = width + PAD
    step_rows = targets * stride
    for block in range(turn_ref.shape[0] // step_rows):
        part = values[:, block * LANES : (block + 1) * LANES]
        turn_ref[pl.ds(block * step_rows + row, targets, stride=stride), :] = part


def store_sums(out_ref, along, bend):
    row = lax.broadcasted_iota(jnp.int32, along.shape, 0)
    value = jnp.where(row < 3, along, bend)
    first = value.astype(BF16).astype(F32)
    second = (value - first).astype(BF16).astype(F32)
    third = value - first - second
    term = jnp.where(row % 3 == 0, first, jnp.where(row % 3 == 1, second, third))
    term = jnp.where(row < 6, term, 0.0).astype(BF16)
    rows = out_ref.shape[1]
    out_ref[:, rows - 8 : rows, :] = jnp.broadcast_to(term[None], (out_ref.shape[0],) + term.shape)


def step_of(back_ref):
    rows = back_ref.shape[1]
    sums = jnp.sum(back_ref[:, rows - 8 : rows, :].astype(F32), axis=0)
    along = sums[0:1, 0:1] + sums[1:2, 0:1] + sums[2:3, 0:1]
    bend = sums[3:4, 0:1] + sums[4:5, 0:1] + sums[5:6, 0:1]
    return along / bend


def back_of(err, weight, half):
    turned = jnp.concatenate([err[half:], -err[:half]], axis=0)
    return dot_nn(err, weight[0]) + dot_nn(turned, weight[1])


GROUP = 8
SLOTS = 3


def group_copies(arrays, buffers, sems, g):
    slot = g % SLOTS
    return [
        pltpu.make_async_copy(array.at[pl.ds(g * GROUP, GROUP)], buffer.at[slot], sems.at[n, slot])
        for n, (array, buffer) in enumerate(zip(arrays, buffers))
    ]


def over_bins(arrays, buffers, sems, one_bin, one_group=None):
    groups = arrays[0].shape[0] // GROUP
    for g in range(min(SLOTS, groups)):
        for copy in group_copies(arrays, buffers, sems, g):
            copy.start()

    def group(g, carry):
        for copy in group_copies(arrays, buffers, sems, g):
            copy.wait()
        for b in range(GROUP):
            slices = [buffer.at[g % SLOTS, b] for buffer in buffers]
            carry = one_bin(g * GROUP + b, *slices, carry)
        if one_group is not None:
            one_group(g, groups)

        @pl.when(g + SLOTS < groups)
        def _():
            for copy in group_copies(arrays, buffers, sems, g + SLOTS):
                copy.start()

        return carry

    return lambda carry: lax.fori_loop(0, groups, group, carry)


def rhs_kernel(
    bright_ref, gains_ref, momentum_ref, factors, w_hbm, target_hbm,
    out_ref, high_ref, low_ref, w_buf, target_buf, back_buf, sems,
):
    bins, _, targets, mics = target_hbm.shape
    bright = jnp.concatenate([bright_ref[...], bright_ref[...]], axis=0) == 1.0

    def one_bin(j, weight, target, carry):
        wanted = target[...].reshape(2 * targets, mics).astype(F32)
        err = jnp.where(bright, wanted, 0.0).astype(BF16)
        back = back_of(err, weight, targets)
        store_bin(back_buf, j, targets, 2 * bins, back[:targets])
        store_bin(back_buf, bins + j, targets, 2 * bins, back[targets:])
        return carry

    def one_group(g, groups):
        each = (factors.shape[0] // 2 - bins) // groups
        for d in range(each):
            table_rows(g * each + d, bins, factors, high_ref, low_ref)

    over_bins((w_hbm, target_hbm), (w_buf, target_buf), sems, one_bin, one_group)(0)
    turn_out(back_buf, out_ref, targets)


def normal_kernel(
    spec_ref, gains_ref, reg_ref, along_ref, w_hbm, out_ref, w_buf, spec_buf, back_buf, sems
):
    bins = w_hbm.shape[0]
    targets = gains_ref.shape[0]

    def one_bin(j, weight, bend):
        real = load_bin(spec_buf, j, targets, 2 * bins)
        imag = load_bin(spec_buf, bins + j, targets, 2 * bins)
        wide = jnp.concatenate([real, imag], axis=0)
        spec = wide.astype(BF16)
        turned = jnp.concatenate([-imag, real], axis=0).astype(BF16)
        press = dot_nt(spec, weight[0]) + dot_nt(turned, weight[1])
        back = back_of((gains * press).astype(BF16), weight, targets)
        back = back + reg_ref[j] * wide
        store_bin(back_buf, j, targets, 2 * bins, back[:targets])
        store_bin(back_buf, bins + j, targets, 2 * bins, back[targets:])
        return bend + wide * back

    run = over_bins((w_hbm,), (w_buf,), sems, one_bin)
    gains = jnp.concatenate([gains_ref[...], gains_ref[...]], axis=0)
    turn_in(spec_ref, spec_buf, targets)
    bend = run(jnp.zeros((2 * targets, w_hbm.shape[3]), F32))
    turn_out(back_buf, out_ref, targets)
    store_sums(out_ref, along_ref[...], jnp.sum(bend))


PIECES = 4


def taps_of(back_ref, high_ref, low_ref, count):
    rows = high_ref.shape[0] // PIECES
    per = back_ref.shape[0] // PIECES
    total = None
    for c in range(PIECES):
        part = pl.ds(c * rows, rows)
        block = jnp.concatenate([back_ref[c * per + d, :count, :] for d in range(per)], axis=1)
        term = dot_nn(block, high_ref[part, :]) + dot_nn(block, low_ref[part, :])
        total = term if total is None else total + term
    return total


def spectrum_to(out_ref, direction, high_ref, low_ref):
    rows = high_ref.shape[0] // PIECES
    per = out_ref.shape[0] // PIECES
    width = out_ref.shape[2]
    count = direction.shape[0]
    high = direction.astype(BF16)
    low = (direction - high.astype(F32)).astype(BF16)
    both = jnp.concatenate([high, low], axis=0)
    for c in range(PIECES):
        part = pl.ds(c * rows, rows)
        wide = dot_nt(both, high_ref[part, :])
        spec = wide[:count] + wide[count:] + dot_nt(high, low_ref[part, :])
        for d in range(per):
            out_ref[c * per + d] = spec[:, d * width : (d + 1) * width].astype(BF16)


def first_kernel(back_ref, high_ref, low_ref, rhs_ref, spec_ref, along_ref):
    rhs = taps_of(back_ref, high_ref, low_ref, rhs_ref.shape[0])
    rhs_ref[...] = rhs
    along_ref[...] = jnp.broadcast_to(jnp.sum(rhs * rhs), along_ref.shape)
    spectrum_to(spec_ref, rhs, high_ref, low_ref)


def middle_kernel(
    back_ref, rhs_ref, momentum_ref, high_ref, low_ref, residual_ref, spec_ref, along_ref, step_ref
):
    step = step_of(back_ref)
    step_ref[...] = jnp.broadcast_to(step, step_ref.shape)
    image = taps_of(back_ref, high_ref, low_ref, residual_ref.shape[0])
    rhs = rhs_ref[...]
    residual = rhs - step * image
    direction = residual + momentum_ref[0:1, 0:1] * rhs
    residual_ref[...] = residual
    along_ref[...] = jnp.broadcast_to(jnp.sum(residual * direction), along_ref.shape)
    spectrum_to(spec_ref, direction, high_ref, low_ref)


def last_kernel(
    back_ref, rhs_ref, residual_ref, step_ref, momentum_ref, high_ref, low_ref,
    filters_out, residual_out,
):
    step = step_of(back_ref)
    rhs = rhs_ref[...]
    residual = residual_ref[...]
    direction = residual + momentum_ref[0:1, 0:1] * rhs
    filters_out[...] = step_ref[0:1, 0:1] * rhs + step * direction
    image = taps_of(back_ref, high_ref, low_ref, residual_ref.shape[0])
    residual_out[...] = residual - step * image


def vmem():
    return pl.BlockSpec(memory_space=pltpu.VMEM)


def smem():
    return pl.BlockSpec(memory_space=pltpu.SMEM)


def hbm():
    return pl.BlockSpec(memory_space=pltpu.HBM)


def kernel_body(transfer, target, zone_mask, dark_weight, reg_weight, momentum):
    bins, _, mics, speakers = transfer.shape
    targets = target.shape[2]
    devices = F // bins
    rows = targets * (speakers // devices)
    block = pltpu.VMEM((devices, rows, 2 * bins), BF16)
    summed = pltpu.VMEM((devices, rows + 8, 2 * bins), BF16)
    tile = jax.ShapeDtypeStruct((8, 128), F32)
    taps = jax.ShapeDtypeStruct((rows, K), F32)
    gains = jnp.where(zone_mask == 1, jnp.float32(1.0), dark_weight[:, None])
    bright = (zone_mask == 1).astype(F32)
    factors = pltpu.with_memory_space_constraint(table_factors(devices, F, K), pltpu.HBM)
    target = pltpu.with_memory_space_constraint(target, pltpu.HBM)
    momentum = jnp.broadcast_to(momentum, (8, 128))
    weights = pltpu.VMEM((SLOTS, GROUP) + transfer.shape[1:], BF16)
    turning = pltpu.VMEM((speakers // LANES * targets * (2 * bins + PAD), LANES), F32)
    sems = pltpu.SemaphoreType.DMA((2, SLOTS))

    def exchange(payload):
        received = lax.all_to_all(payload, AXES, split_axis=0, concat_axis=0, tiled=True)
        return pltpu.with_memory_space_constraint(received, pltpu.VMEM)

    def call(kernel, name, in_specs, out_shape, scratch=()):
        return pl.pallas_call(
            kernel,
            in_specs=in_specs,
            out_specs=jax.tree.map(lambda _: vmem(), out_shape),
            out_shape=out_shape,
            scratch_shapes=scratch,
            compiler_params=pltpu.CompilerParams(vmem_limit_bytes=VMEM_BYTES),
            name=name,
        )

    normal = call(
        normal_kernel, "normal", [vmem(), vmem(), smem(), vmem(), hbm()],
        summed, [weights, turning, turning, sems],
    )
    table = pltpu.VMEM((2 * F, K), BF16)
    wanted = pltpu.VMEM((SLOTS, GROUP) + target.shape[1:], BF16)
    back, high, low = call(
        rhs_kernel, "rhs_back", [vmem()] * 4 + [hbm(), hbm()], [block, table, table],
        [weights, wanted, turning, sems],
    )(bright, gains, momentum, factors, transfer, target)
    high = pltpu.with_memory_space_constraint(high, pltpu.VMEM)
    low = pltpu.with_memory_space_constraint(low, pltpu.VMEM)
    rhs, spec, along = call(first_kernel, "first_taps", [vmem()] * 3, [taps, block, tile])(
        exchange(back), high, low
    )
    back = normal(exchange(spec), gains, reg_weight, along, transfer)
    residual, spec, along, step = call(
        middle_kernel, "middle_taps", [vmem()] * 5, [taps, block, tile, tile],
    )(exchange(back), rhs, momentum, high, low)
    back = normal(exchange(spec), gains, reg_weight, along, transfer)
    filters, residual = call(
        last_kernel, "last_taps", [vmem()] * 7, [taps, taps]
    )(exchange(back), rhs, residual, step, momentum, high, low)
    shape = (targets, speakers // devices, K)
    return filters.reshape(shape), residual.reshape(shape)


def body(transfer, target, *rest):
    bins, _, mics, speakers = transfer.shape
    devices = F // bins
    whole_tiles = (
        bins == 64
        and speakers == 8 * devices
        and speakers % 128 == 0
        and mics % 128 == 0
        and target.shape[2] == 32
        and devices % 4 == 0
    )
    return (kernel_body if whole_tiles else plain_body)(transfer, target, *rest)


def solution(mesh):
    in_specs = (
        P(AXES, None, None, None),
        P(AXES, None, None, None),
        P(),
        P(),
        P(AXES),
        P(),
    )
    out_specs = (P(None, AXES, None), P(None, AXES, None))
    return jax.shard_map(body, mesh=mesh, in_specs=in_specs, out_specs=out_specs, check_vma=False)
```

```python
import math

import jax
import jax.numpy as jnp
import numpy as np
from jax import lax
from jax.experimental import pallas as pl
from jax.experimental.pallas import tpu as pltpu
from jax.sharding import PartitionSpec as P

K = 1024
F = 2048
ITERS = 2
AXES = ("row", "col")
BF16 = jnp.bfloat16
F32 = jnp.float32
NT = (((1,), (1,)), ((), ()))
VMEM_BYTES = 28 * 2**20


def dot_nn(a, b):
    return jnp.dot(a, b, preferred_element_type=F32)


def dot_nt(a, b):
    return lax.dot_general(a, b, NT, preferred_element_type=F32)


def build_table(taps, bins):
    tap_index = jnp.arange(taps, dtype=jnp.int32)[:, None]
    bin_index = jnp.arange(bins, dtype=jnp.int32)[None, :]
    phase = (tap_index * bin_index % bins).astype(jnp.float32) * (2.0 * math.pi / bins)
    return jnp.stack([jnp.cos(phase), -jnp.sin(phase)], axis=1) / math.sqrt(bins)


def plain_body(transfer, target, zone_mask, dark_weight, reg_weight, momentum):
    dft_table = build_table(K, F)
    mic_gains = jnp.where(zone_mask == 1, jnp.float32(1.0), dark_weight[:, None])
    weight_real = transfer[:, 0]
    weight_imag = transfer[:, 1]
    reg_term = reg_weight[:, None, None]

    def to_taps(spectrum):
        regrouped = lax.all_to_all(spectrum, AXES, split_axis=3, concat_axis=0, tiled=True)
        return jnp.einsum("fctl,kcf->tlk", regrouped, dft_table, precision=lax.Precision.HIGHEST)

    def contract(spec, first, second):
        return jnp.einsum(spec, first, second, preferred_element_type=jnp.float32)

    def back_project(err_real, err_imag):
        spec = "fml,ftm->ftl"
        back_real = contract(spec, weight_real, err_real) + contract(spec, weight_imag, err_imag)
        back_imag = contract(spec, weight_real, err_imag) - contract(spec, weight_imag, err_real)
        return back_real, back_imag

    rhs_error = jnp.where(zone_mask[None, None] == 1, target, jnp.zeros_like(target))
    rhs = to_taps(jnp.stack(back_project(rhs_error[:, 0], rhs_error[:, 1]), axis=1))
    filters = jnp.zeros_like(rhs)
    residual = rhs
    direction = rhs
    for iteration in range(ITERS):
        along_term = jnp.sum(residual * direction)
        to_spectrum = jnp.einsum(
            "tlk,kcf->fctl", direction, dft_table, precision=lax.Precision.HIGHEST
        ).astype(jnp.bfloat16)
        spec = lax.all_to_all(to_spectrum, AXES, split_axis=0, concat_axis=3, tiled=True)
        spec_real = spec[:, 0]
        spec_imag = spec[:, 1]
        form = "fml,ftl->ftm"
        press_real = contract(form, weight_real, spec_real) - contract(form, weight_imag, spec_imag)
        press_imag = contract(form, weight_real, spec_imag) + contract(form, weight_imag, spec_real)
        back_real, back_imag = back_project(
            (mic_gains * press_real).astype(jnp.bfloat16),
            (mic_gains * press_imag).astype(jnp.bfloat16),
        )
        image_taps = to_taps(
            jnp.stack(
                [
                    back_real + reg_term * spec_real.astype(jnp.float32),
                    back_imag + reg_term * spec_imag.astype(jnp.float32),
                ],
                axis=1,
            )
        )
        along_sum, bend_sum = lax.psum((along_term, jnp.sum(direction * image_taps)), AXES)
        step_size = along_sum / bend_sum
        filters = filters + step_size * direction
        residual = residual - step_size * image_taps
        if iteration + 1 < ITERS:
            direction = residual + momentum[iteration] * direction
    return (filters, residual)


def table_factors(devices, bins, taps):
    local = bins // devices
    tap = np.arange(taps)
    scale = 2.0 * math.pi / bins
    coarse = (np.arange(devices // 2)[:, None] * local * tap[None, :]) % bins * scale
    fine = (np.arange(local)[:, None] * tap[None, :]) % bins * scale
    norm = 1.0 / math.sqrt(bins)
    factors = (np.cos(coarse) * norm, np.sin(coarse) * norm, np.cos(fine), np.sin(fine))
    return jnp.asarray(np.concatenate(factors).astype(np.float32))


def table_rows(d, bins, factors, high_ref, low_ref):
    half = factors.shape[0] // 2 - bins
    cos_c = factors[pl.ds(d, 1), :]
    sin_c = factors[pl.ds(half + d, 1), :]
    cos_f = factors[2 * half : 2 * half + bins, :]
    sin_f = factors[2 * half + bins :, :]
    odd = lax.broadcasted_iota(jnp.int32, cos_f.shape, 1) % 2
    sign = (1 - 2 * odd).astype(BF16)
    parts = (cos_c * cos_f - sin_c * sin_f, -(sin_c * cos_f + cos_c * sin_f))
    for c, value in enumerate(parts):
        high = value.astype(BF16)
        low = (value - high.astype(F32)).astype(BF16)
        here = pl.ds((2 * d + c) * bins, bins)
        there = pl.ds((2 * (d + half) + c) * bins, bins)
        high_ref[here, :] = high
        low_ref[here, :] = low
        high_ref[there, :] = high * sign
        low_ref[there, :] = low * sign


LANES = 128
PAD = 8


def turn_out(turn_ref, out_ref, targets):
    devices, _, width = out_ref.shape
    pitch = width + PAD
    step_rows = targets * pitch
    blocks = turn_ref.shape[0] // step_rows
    each = devices // blocks

    def step(pair, carry):
        for block in range(blocks):
            halves = []
            for side in range(2):
                start = block * step_rows + (2 * pair + side) * pitch
                halves.append(turn_ref[pl.ds(start, width), :].T.reshape(each, 8, width))
            both = jnp.concatenate(halves, axis=1).astype(BF16)
            out_ref[block * each : (block + 1) * each, pl.ds(16 * pair, 16), :] = both
        return carry

    lax.fori_loop(0, targets // 2, step, 0)


def turn_in(in_ref, turn_ref, targets):
    devices, _, width = in_ref.shape
    pitch = width + PAD
    step_rows = targets * pitch
    blocks = turn_ref.shape[0] // step_rows
    each = devices // blocks

    def step(pair, carry):
        for block in range(blocks):
            part = in_ref[block * each : (block + 1) * each, pl.ds(16 * pair, 16), :].astype(F32)
            for side in range(2):
                half = part[:, 8 * side : 8 * side + 8, :].reshape(LANES, width)
                start = block * step_rows + (2 * pair + side) * pitch
                turn_ref[pl.ds(start, width), :] = half.T
        return carry

    lax.fori_loop(0, targets // 2, step, 0)


def load_bin(turn_ref, row, targets, width):
    stride = width + PAD
    step_rows = targets * stride
    return jnp.concatenate(
        [
            turn_ref[pl.ds(block * step_rows + row, targets, stride=stride), :]
            for block in range(turn_ref.shape[0] // step_rows)
        ],
        axis=1,
    )


def store_bin(turn_ref, row, targets, width, values):
    stride = width + PAD
    step_rows = targets * stride
    for block in range(turn_ref.shape[0] // step_rows):
        part = values[:, block * LANES : (block + 1) * LANES]
        turn_ref[pl.ds(block * step_rows + row, targets, stride=stride), :] = part


def store_sums(out_ref, along, bend):
    row = lax.broadcasted_iota(jnp.int32, along.shape, 0)
    value = jnp.where(row < 3, along, bend)
    first = value.astype(BF16).astype(F32)
    second = (value - first).astype(BF16).astype(F32)
    third = value - first - second
    term = jnp.where(row % 3 == 0, first, jnp.where(row % 3 == 1, second, third))
    term = jnp.where(row < 6, term, 0.0).astype(BF16)
    rows = out_ref.shape[1]
    out_ref[:, rows - 8 : rows, :] = jnp.broadcast_to(term[None], (out_ref.shape[0],) + term.shape)


def step_of(back_ref):
    rows = back_ref.shape[1]
    sums = jnp.sum(back_ref[:, rows - 8 : rows, :].astype(F32), axis=0)
    along = sums[0:1, 0:1] + sums[1:2, 0:1] + sums[2:3, 0:1]
    bend = sums[3:4, 0:1] + sums[4:5, 0:1] + sums[5:6, 0:1]
    return along / bend


def back_of(err, weight, half):
    turned = jnp.concatenate([err[half:], -err[:half]], axis=0)
    return dot_nn(err, weight[0]) + dot_nn(turned, weight[1])


GROUP = 8
SLOTS = 3
AHEAD = 2


def group_copies(arrays, buffers, sems, g):
    slot = g % SLOTS
    return [
        pltpu.make_async_copy(array.at[pl.ds(g * GROUP, GROUP)], buffer.at[slot], sems.at[n, slot])
        for n, (array, buffer) in enumerate(zip(arrays, buffers))
    ]


def over_bins(arrays, buffers, sems, prepare, one_bin, one_group=None):
    groups = arrays[0].shape[0] // GROUP
    for g in range(min(SLOTS, groups)):
        for copy in group_copies(arrays, buffers, sems, g):
            copy.start()

    def group(g, carry):
        for copy in group_copies(arrays, buffers, sems, g):
            copy.wait()
        slices = [[buffer.at[g % SLOTS, b] for buffer in buffers] for b in range(GROUP)]
        begun = [prepare(g * GROUP + b, *slices[b]) for b in range(AHEAD)]
        for b in range(GROUP):
            if b + AHEAD < GROUP:
                begun.append(prepare(g * GROUP + b + AHEAD, *slices[b + AHEAD]))
            carry = one_bin(g * GROUP + b, *slices[b], begun[b], carry)
        if one_group is not None:
            one_group(g)

        @pl.when(g + SLOTS < groups)
        def _():
            for copy in group_copies(arrays, buffers, sems, g + SLOTS):
                copy.start()

        return carry

    return lambda carry: lax.fori_loop(0, groups, group, carry)


def rhs_kernel(
    bright_ref, gains_ref, momentum_ref, factors, w_hbm, target_hbm,
    out_ref, high_ref, low_ref, w_buf, target_buf, back_buf, sems,
):
    bins, _, targets, mics = target_hbm.shape
    bright = jnp.concatenate([bright_ref[...], bright_ref[...]], axis=0).astype(BF16)

    def prepare(j, weight, target):
        return target[...].reshape(2 * targets, mics) * bright

    def one_bin(j, weight, target, err, carry):
        back = back_of(err, weight, targets)
        store_bin(back_buf, j, targets, 2 * bins, back[:targets])
        store_bin(back_buf, bins + j, targets, 2 * bins, back[targets:])
        return carry

    half = factors.shape[0] // 2 - bins
    groups = bins // GROUP
    first = half // 2
    each = (half - first) // groups

    def one_group(g):
        for d in range(each):
            table_rows(first + g * each + d, bins, factors, high_ref, low_ref)

    run = over_bins((w_hbm, target_hbm), (w_buf, target_buf), sems, prepare, one_bin, one_group)
    for d in range(first):
        table_rows(d, bins, factors, high_ref, low_ref)
    run(0)
    turn_out(back_buf, out_ref, targets)


def normal_kernel(
    spec_ref, gains_ref, reg_ref, along_ref, w_hbm, out_ref, w_buf, spec_buf, back_buf, sems
):
    bins = w_hbm.shape[0]
    targets = gains_ref.shape[0]

    def prepare(j, weight):
        real = load_bin(spec_buf, j, targets, 2 * bins)
        imag = load_bin(spec_buf, bins + j, targets, 2 * bins)
        wide = jnp.concatenate([real, imag], axis=0)
        spec = wide.astype(BF16)
        turned = jnp.concatenate([-imag, real], axis=0).astype(BF16)
        press = dot_nt(spec, weight[0]) + dot_nt(turned, weight[1])
        return wide, (gains * press).astype(BF16)

    def one_bin(j, weight, prepared, bend):
        wide, err = prepared
        back = back_of(err, weight, targets)
        back = back + reg_ref[j] * wide
        store_bin(back_buf, j, targets, 2 * bins, back[:targets])
        store_bin(back_buf, bins + j, targets, 2 * bins, back[targets:])
        return bend + wide * back

    run = over_bins((w_hbm,), (w_buf,), sems, prepare, one_bin)
    gains = jnp.concatenate([gains_ref[...], gains_ref[...]], axis=0)
    turn_in(spec_ref, spec_buf, targets)
    bend = run(jnp.zeros((2 * targets, w_hbm.shape[3]), F32))
    turn_out(back_buf, out_ref, targets)
    store_sums(out_ref, along_ref[...], jnp.sum(bend))


PIECES = 4


def taps_of(back_ref, high_ref, low_ref, count):
    rows = high_ref.shape[0] // PIECES
    per = back_ref.shape[0] // PIECES
    total = None
    for c in range(PIECES):
        part = pl.ds(c * rows, rows)
        block = jnp.concatenate([back_ref[c * per + d, :count, :] for d in range(per)], axis=1)
        term = dot_nn(block, high_ref[part, :]) + dot_nn(block, low_ref[part, :])
        total = term if total is None else total + term
    return total


def mirror_matrix(bins):
    row = lax.broadcasted_iota(jnp.int32, (4 * bins, 2 * bins), 0)
    col = lax.broadcasted_iota(jnp.int32, (4 * bins, 2 * bins), 1)
    part = col // bins
    place = col % bins
    source = jnp.where(place == 0, (2 + part) * bins, part * bins + bins - place)
    sign = (1 - 2 * part).astype(F32)
    return jnp.where(row == source, sign, 0.0).astype(BF16)


def spectrum_to(out_ref, direction, high_ref, low_ref):
    devices, _, width = out_ref.shape
    half = devices // 2
    per = half // (PIECES // 2)
    count = direction.shape[0]
    high = direction.astype(BF16)
    low = (direction - high.astype(F32)).astype(BF16)
    both = jnp.concatenate([high, low], axis=0)
    mirror = mirror_matrix(width // 2)

    def blocks(first, number):
        part = pl.ds(first * width, number * width)
        wide = dot_nt(both, high_ref[part, :])
        spec = wide[:count] + wide[count:] + dot_nt(high, low_ref[part, :])
        return spec.astype(BF16)

    after = blocks(half, 1)
    for c in reversed(range(half // per)):
        spec = blocks(c * per, per)
        wider = jnp.concatenate([spec, after], axis=1)
        for d in range(per):
            here = c * per + d
            out_ref[here] = spec[:, d * width : (d + 1) * width]
            pair = wider[:, d * width : (d + 2) * width]
            out_ref[devices - 1 - here] = dot_nn(pair, mirror).astype(BF16)
        after = spec[:, :width]


def first_kernel(back_ref, high_ref, low_ref, rhs_ref, spec_ref, along_ref):
    rhs = taps_of(back_ref, high_ref, low_ref, rhs_ref.shape[0])
    rhs_ref[...] = rhs
    along_ref[...] = jnp.broadcast_to(jnp.sum(rhs * rhs), along_ref.shape)
    spectrum_to(spec_ref, rhs, high_ref, low_ref)


def middle_kernel(
    back_ref, rhs_ref, momentum_ref, high_ref, low_ref, residual_ref, spec_ref, along_ref, step_ref
):
    step = step_of(back_ref)
    step_ref[...] = jnp.broadcast_to(step, step_ref.shape)
    image = taps_of(back_ref, high_ref, low_ref, residual_ref.shape[0])
    rhs = rhs_ref[...]
    residual = rhs - step * image
    direction = residual + momentum_ref[0:1, 0:1] * rhs
    residual_ref[...] = residual
    along_ref[...] = jnp.broadcast_to(jnp.sum(residual * direction), along_ref.shape)
    spectrum_to(spec_ref, direction, high_ref, low_ref)


def last_kernel(
    back_ref, rhs_ref, residual_ref, step_ref, momentum_ref, high_ref, low_ref,
    filters_out, residual_out,
):
    step = step_of(back_ref)
    rhs = rhs_ref[...]
    residual = residual_ref[...]
    direction = residual + momentum_ref[0:1, 0:1] * rhs
    filters_out[...] = step_ref[0:1, 0:1] * rhs + step * direction
    image = taps_of(back_ref, high_ref, low_ref, residual_ref.shape[0])
    residual_out[...] = residual - step * image


def vmem():
    return pl.BlockSpec(memory_space=pltpu.VMEM)


def smem():
    return pl.BlockSpec(memory_space=pltpu.SMEM)


def hbm():
    return pl.BlockSpec(memory_space=pltpu.HBM)


def kernel_body(transfer, target, zone_mask, dark_weight, reg_weight, momentum):
    bins, _, mics, speakers = transfer.shape
    targets = target.shape[2]
    devices = F // bins
    rows = targets * (speakers // devices)
    block = pltpu.VMEM((devices, rows, 2 * bins), BF16)
    summed = pltpu.VMEM((devices, rows + 8, 2 * bins), BF16)
    tile = jax.ShapeDtypeStruct((8, 128), F32)
    taps = jax.ShapeDtypeStruct((rows, K), F32)
    gains = jnp.where(zone_mask == 1, jnp.float32(1.0), dark_weight[:, None])
    bright = (zone_mask == 1).astype(F32)
    factors = pltpu.with_memory_space_constraint(table_factors(devices, F, K), pltpu.HBM)
    target = pltpu.with_memory_space_constraint(target, pltpu.HBM)
    momentum = jnp.broadcast_to(momentum, (8, 128))
    weights = pltpu.VMEM((SLOTS, GROUP) + transfer.shape[1:], BF16)
    turning = pltpu.VMEM((speakers // LANES * targets * (2 * bins + PAD), LANES), F32)
    sems = pltpu.SemaphoreType.DMA((2, SLOTS))

    def exchange(payload):
        received = lax.all_to_all(payload, AXES, split_axis=0, concat_axis=0, tiled=True)
        return pltpu.with_memory_space_constraint(received, pltpu.VMEM)

    def call(kernel, name, in_specs, out_shape, scratch=()):
        return pl.pallas_call(
            kernel,
            in_specs=in_specs,
            out_specs=jax.tree.map(lambda _: vmem(), out_shape),
            out_shape=out_shape,
            scratch_shapes=scratch,
            compiler_params=pltpu.CompilerParams(vmem_limit_bytes=VMEM_BYTES),
            name=name,
        )

    normal = call(
        normal_kernel, "normal", [vmem(), vmem(), smem(), vmem(), hbm()],
        summed, [weights, turning, turning, sems],
    )
    table = pltpu.VMEM((2 * F, K), BF16)
    wanted = pltpu.VMEM((SLOTS, GROUP) + target.shape[1:], BF16)
    back, high, low = call(
        rhs_kernel, "rhs_back", [vmem()] * 4 + [hbm(), hbm()], [block, table, table],
        [weights, wanted, turning, sems],
    )(bright, gains, momentum, factors, transfer, target)
    high = pltpu.with_memory_space_constraint(high, pltpu.VMEM)
    low = pltpu.with_memory_space_constraint(low, pltpu.VMEM)
    rhs, spec, along = call(first_kernel, "first_taps", [vmem()] * 3, [taps, block, tile])(
        exchange(back), high, low
    )
    back = normal(exchange(spec), gains, reg_weight, along, transfer)
    residual, spec, along, step = call(
        middle_kernel, "middle_taps", [vmem()] * 5, [taps, block, tile, tile],
    )(exchange(back), rhs, momentum, high, low)
    back = normal(exchange(spec), gains, reg_weight, along, transfer)
    filters, residual = call(
        last_kernel, "last_taps", [vmem()] * 7, [taps, taps]
    )(exchange(back), rhs, residual, step, momentum, high, low)
    shape = (targets, speakers // devices, K)
    return filters.reshape(shape), residual.reshape(shape)


def body(transfer, target, *rest):
    bins, _, mics, speakers = transfer.shape
    devices = F // bins
    whole_tiles = (
        bins == 64
        and speakers == 8 * devices
        and speakers % 128 == 0
        and mics % 128 == 0
        and target.shape[2] == 32
        and devices % 4 == 0
    )
    return (kernel_body if whole_tiles else plain_body)(transfer, target, *rest)


def solution(mesh):
    in_specs = (
        P(AXES, None, None, None),
        P(AXES, None, None, None),
        P(),
        P(),
        P(AXES),
        P(),
    )
    out_specs = (P(None, AXES, None), P(None, AXES, None))
    return jax.shard_map(body, mesh=mesh, in_specs=in_specs, out_specs=out_specs, check_vma=False)
```

```python
import math

import jax
import jax.numpy as jnp
import numpy as np
from jax import lax
from jax.experimental import pallas as pl
from jax.experimental.pallas import tpu as pltpu
from jax.sharding import PartitionSpec as P

K = 1024
F = 2048
ITERS = 2
AXES = ("row", "col")
BF16 = jnp.bfloat16
F32 = jnp.float32
NT = (((1,), (1,)), ((), ()))
VMEM_BYTES = 28 * 2**20


def dot_nn(a, b):
    return jnp.dot(a, b, preferred_element_type=F32)


def dot_nt(a, b):
    return lax.dot_general(a, b, NT, preferred_element_type=F32)


def build_table(taps, bins):
    tap_index = jnp.arange(taps, dtype=jnp.int32)[:, None]
    bin_index = jnp.arange(bins, dtype=jnp.int32)[None, :]
    phase = (tap_index * bin_index % bins).astype(jnp.float32) * (2.0 * math.pi / bins)
    return jnp.stack([jnp.cos(phase), -jnp.sin(phase)], axis=1) / math.sqrt(bins)


def plain_body(transfer, target, zone_mask, dark_weight, reg_weight, momentum):
    dft_table = build_table(K, F)
    mic_gains = jnp.where(zone_mask == 1, jnp.float32(1.0), dark_weight[:, None])
    weight_real = transfer[:, 0]
    weight_imag = transfer[:, 1]
    reg_term = reg_weight[:, None, None]

    def to_taps(spectrum):
        regrouped = lax.all_to_all(spectrum, AXES, split_axis=3, concat_axis=0, tiled=True)
        return jnp.einsum("fctl,kcf->tlk", regrouped, dft_table, precision=lax.Precision.HIGHEST)

    def contract(spec, first, second):
        return jnp.einsum(spec, first, second, preferred_element_type=jnp.float32)

    def back_project(err_real, err_imag):
        spec = "fml,ftm->ftl"
        back_real = contract(spec, weight_real, err_real) + contract(spec, weight_imag, err_imag)
        back_imag = contract(spec, weight_real, err_imag) - contract(spec, weight_imag, err_real)
        return back_real, back_imag

    rhs_error = jnp.where(zone_mask[None, None] == 1, target, jnp.zeros_like(target))
    rhs = to_taps(jnp.stack(back_project(rhs_error[:, 0], rhs_error[:, 1]), axis=1))
    filters = jnp.zeros_like(rhs)
    residual = rhs
    direction = rhs
    for iteration in range(ITERS):
        along_term = jnp.sum(residual * direction)
        to_spectrum = jnp.einsum(
            "tlk,kcf->fctl", direction, dft_table, precision=lax.Precision.HIGHEST
        ).astype(jnp.bfloat16)
        spec = lax.all_to_all(to_spectrum, AXES, split_axis=0, concat_axis=3, tiled=True)
        spec_real = spec[:, 0]
        spec_imag = spec[:, 1]
        form = "fml,ftl->ftm"
        press_real = contract(form, weight_real, spec_real) - contract(form, weight_imag, spec_imag)
        press_imag = contract(form, weight_real, spec_imag) + contract(form, weight_imag, spec_real)
        back_real, back_imag = back_project(
            (mic_gains * press_real).astype(jnp.bfloat16),
            (mic_gains * press_imag).astype(jnp.bfloat16),
        )
        image_taps = to_taps(
            jnp.stack(
                [
                    back_real + reg_term * spec_real.astype(jnp.float32),
                    back_imag + reg_term * spec_imag.astype(jnp.float32),
                ],
                axis=1,
            )
        )
        along_sum, bend_sum = lax.psum((along_term, jnp.sum(direction * image_taps)), AXES)
        step_size = along_sum / bend_sum
        filters = filters + step_size * direction
        residual = residual - step_size * image_taps
        if iteration + 1 < ITERS:
            direction = residual + momentum[iteration] * direction
    return (filters, residual)


def table_factors(devices, bins, taps):
    local = bins // devices
    tap = np.arange(taps)
    scale = 2.0 * math.pi / bins
    coarse = (np.arange(devices // 2)[:, None] * local * tap[None, :]) % bins * scale
    fine = (np.arange(local)[:, None] * tap[None, :]) % bins * scale
    norm = 1.0 / math.sqrt(bins)
    factors = (np.cos(coarse) * norm, np.sin(coarse) * norm, np.cos(fine), np.sin(fine))
    return jnp.asarray(np.concatenate(factors).astype(np.float32))


def table_rows(d, bins, factors, high_ref, low_ref):
    half = factors.shape[0] // 2 - bins
    cos_c = factors[pl.ds(d, 1), :]
    sin_c = factors[pl.ds(half + d, 1), :]
    cos_f = factors[2 * half : 2 * half + bins, :]
    sin_f = factors[2 * half + bins :, :]
    odd = lax.broadcasted_iota(jnp.int32, cos_f.shape, 1) % 2
    sign = (1 - 2 * odd).astype(BF16)
    parts = (cos_c * cos_f - sin_c * sin_f, -(sin_c * cos_f + cos_c * sin_f))
    for c, value in enumerate(parts):
        high = value.astype(BF16)
        low = (value - high.astype(F32)).astype(BF16)
        here = pl.ds((2 * d + c) * bins, bins)
        there = pl.ds((2 * (d + half) + c) * bins, bins)
        high_ref[here, :] = high
        low_ref[here, :] = low
        high_ref[there, :] = high * sign
        low_ref[there, :] = low * sign


LANES = 128
PAD = 8


def turn_out(turn_ref, out_ref, targets):
    devices, _, width = out_ref.shape
    pitch = width + PAD
    step_rows = targets * pitch
    blocks = turn_ref.shape[0] // step_rows
    each = devices // blocks

    def step(pair, carry):
        for block in range(blocks):
            halves = []
            for side in range(2):
                start = block * step_rows + (2 * pair + side) * pitch
                halves.append(turn_ref[pl.ds(start, width), :].T.reshape(each, 8, width))
            both = jnp.concatenate(halves, axis=1).astype(BF16)
            out_ref[block * each : (block + 1) * each, pl.ds(16 * pair, 16), :] = both
        return carry

    lax.fori_loop(0, targets // 2, step, 0)


def turn_in(in_ref, turn_ref, targets):
    devices, _, width = in_ref.shape
    pitch = width + PAD
    step_rows = targets * pitch
    blocks = turn_ref.shape[0] // step_rows
    each = devices // blocks

    def step(pair, carry):
        for block in range(blocks):
            part = in_ref[block * each : (block + 1) * each, pl.ds(16 * pair, 16), :].astype(F32)
            for side in range(2):
                half = part[:, 8 * side : 8 * side + 8, :].reshape(LANES, width)
                start = block * step_rows + (2 * pair + side) * pitch
                turn_ref[pl.ds(start, width), :] = half.T
        return carry

    lax.fori_loop(0, targets // 2, step, 0)


def load_bin(turn_ref, row, targets, width):
    stride = width + PAD
    step_rows = targets * stride
    return jnp.concatenate(
        [
            turn_ref[pl.ds(block * step_rows + row, targets, stride=stride), :]
            for block in range(turn_ref.shape[0] // step_rows)
        ],
        axis=1,
    )


def store_bin(turn_ref, row, targets, width, values):
    stride = width + PAD
    step_rows = targets * stride
    for block in range(turn_ref.shape[0] // step_rows):
        part = values[:, block * LANES : (block + 1) * LANES]
        turn_ref[pl.ds(block * step_rows + row, targets, stride=stride), :] = part


def store_sums(out_ref, along, bend):
    row = lax.broadcasted_iota(jnp.int32, along.shape, 0)
    value = jnp.where(row < 3, along, bend)
    first = value.astype(BF16).astype(F32)
    second = (value - first).astype(BF16).astype(F32)
    third = value - first - second
    term = jnp.where(row % 3 == 0, first, jnp.where(row % 3 == 1, second, third))
    term = jnp.where(row < 6, term, 0.0).astype(BF16)
    rows = out_ref.shape[1]
    out_ref[:, rows - 8 : rows, :] = jnp.broadcast_to(term[None], (out_ref.shape[0],) + term.shape)


def step_of(back_ref):
    rows = back_ref.shape[1]
    sums = jnp.sum(back_ref[:, rows - 8 : rows, :].astype(F32), axis=0)
    along = sums[0:1, 0:1] + sums[1:2, 0:1] + sums[2:3, 0:1]
    bend = sums[3:4, 0:1] + sums[4:5, 0:1] + sums[5:6, 0:1]
    return along / bend


def back_of(err, weight, half):
    turned = jnp.concatenate([err[half:], -err[:half]], axis=0)
    return dot_nn(err, weight[0]) + dot_nn(turned, weight[1])


GROUP = 8
SLOTS = 3
AHEAD = 2


def group_copies(arrays, buffers, sems, g):
    slot = g % SLOTS
    return [
        pltpu.make_async_copy(array.at[pl.ds(g * GROUP, GROUP)], buffer.at[slot], sems.at[n, slot])
        for n, (array, buffer) in enumerate(zip(arrays, buffers))
    ]


def over_bins(arrays, buffers, sems, prepare, one_bin, one_group=None):
    groups = arrays[0].shape[0] // GROUP
    for g in range(min(SLOTS, groups)):
        for copy in group_copies(arrays, buffers, sems, g):
            copy.start()

    def group(g, carry):
        for copy in group_copies(arrays, buffers, sems, g):
            copy.wait()
        slices = [[buffer.at[g % SLOTS, b] for buffer in buffers] for b in range(GROUP)]
        begun = [prepare(g * GROUP + b, *slices[b]) for b in range(AHEAD)]
        for b in range(GROUP):
            if b + AHEAD < GROUP:
                begun.append(prepare(g * GROUP + b + AHEAD, *slices[b + AHEAD]))
            carry = one_bin(g * GROUP + b, *slices[b], begun[b], carry)
        if one_group is not None:
            one_group(g)

        @pl.when(g + SLOTS < groups)
        def _():
            for copy in group_copies(arrays, buffers, sems, g + SLOTS):
                copy.start()

        return carry

    return lambda carry: lax.fori_loop(0, groups, group, carry)


def rhs_kernel(
    bright_ref, gains_ref, momentum_ref, factors, w_hbm, target_hbm,
    out_ref, high_ref, low_ref, w_buf, target_buf, back_buf, sems,
):
    bins, _, targets, mics = target_hbm.shape
    bright = jnp.concatenate([bright_ref[...], bright_ref[...]], axis=0).astype(BF16)

    def prepare(j, weight, target):
        return target[...].reshape(2 * targets, mics) * bright

    def one_bin(j, weight, target, err, carry):
        back = back_of(err, weight, targets)
        store_bin(back_buf, j, targets, 2 * bins, back[:targets])
        store_bin(back_buf, bins + j, targets, 2 * bins, back[targets:])
        return carry

    half = factors.shape[0] // 2 - bins
    groups = bins // GROUP
    first = half // 2
    each = (half - first) // groups

    def one_group(g):
        for d in range(each):
            table_rows(first + g * each + d, bins, factors, high_ref, low_ref)

    run = over_bins((w_hbm, target_hbm), (w_buf, target_buf), sems, prepare, one_bin, one_group)
    for d in range(first):
        table_rows(d, bins, factors, high_ref, low_ref)
    run(0)
    turn_out(back_buf, out_ref, targets)


def normal_kernel(
    spec_ref, gains_ref, reg_ref, along_ref, w_hbm, out_ref, w_buf, spec_buf, back_buf, sems
):
    bins = w_hbm.shape[0]
    targets = gains_ref.shape[0]

    def prepare(j, weight):
        real = load_bin(spec_buf, j, targets, 2 * bins)
        imag = load_bin(spec_buf, bins + j, targets, 2 * bins)
        wide = jnp.concatenate([real, imag], axis=0)
        spec = wide.astype(BF16)
        turned = jnp.concatenate([-imag, real], axis=0).astype(BF16)
        press = dot_nt(spec, weight[0]) + dot_nt(turned, weight[1])
        return wide, (gains * press).astype(BF16)

    def one_bin(j, weight, prepared, bend):
        wide, err = prepared
        back = back_of(err, weight, targets)
        back = back + reg_ref[j] * wide
        store_bin(back_buf, j, targets, 2 * bins, back[:targets])
        store_bin(back_buf, bins + j, targets, 2 * bins, back[targets:])
        return bend + wide * back

    run = over_bins((w_hbm,), (w_buf,), sems, prepare, one_bin)
    gains = jnp.concatenate([gains_ref[...], gains_ref[...]], axis=0)
    turn_in(spec_ref, spec_buf, targets)
    bend = run(jnp.zeros((2 * targets, w_hbm.shape[3]), F32))
    turn_out(back_buf, out_ref, targets)
    store_sums(out_ref, along_ref[...], jnp.sum(bend))


PIECES = 2


def taps_of(back_ref, high_ref, low_ref, count):
    rows = high_ref.shape[0] // PIECES
    per = back_ref.shape[0] // PIECES
    total = None
    for c in range(PIECES):
        part = pl.ds(c * rows, rows)
        block = jnp.concatenate([back_ref[c * per + d, :count, :] for d in range(per)], axis=1)
        term = dot_nn(block, high_ref[part, :]) + dot_nn(block, low_ref[part, :])
        total = term if total is None else total + term
    return total


def mirror_matrix(bins):
    row = lax.broadcasted_iota(jnp.int32, (4 * bins, 2 * bins), 0)
    col = lax.broadcasted_iota(jnp.int32, (4 * bins, 2 * bins), 1)
    part = col // bins
    place = col % bins
    source = jnp.where(place == 0, (2 + part) * bins, part * bins + bins - place)
    sign = (1 - 2 * part).astype(F32)
    return jnp.where(row == source, sign, 0.0).astype(BF16)


def spectrum_to(out_ref, direction, high_ref, low_ref):
    devices, _, width = out_ref.shape
    half = devices // 2
    per = half // (PIECES // 2)
    count = direction.shape[0]
    high = direction.astype(BF16)
    low = (direction - high.astype(F32)).astype(BF16)
    both = jnp.concatenate([high, low], axis=0)
    mirror = mirror_matrix(width // 2)

    def blocks(first, number):
        part = pl.ds(first * width, number * width)
        wide = dot_nt(both, high_ref[part, :])
        spec = wide[:count] + wide[count:] + dot_nt(high, low_ref[part, :])
        return spec.astype(BF16)

    after = blocks(half, 1)
    for c in reversed(range(half // per)):
        spec = blocks(c * per, per)
        wider = jnp.concatenate([spec, after], axis=1)
        for d in range(per):
            here = c * per + d
            out_ref[here] = spec[:, d * width : (d + 1) * width]
            pair = wider[:, d * width : (d + 2) * width]
            out_ref[devices - 1 - here] = dot_nn(pair, mirror).astype(BF16)
        after = spec[:, :width]


def first_kernel(back_ref, high_ref, low_ref, rhs_ref, spec_ref, along_ref):
    rhs = taps_of(back_ref, high_ref, low_ref, rhs_ref.shape[0])
    rhs_ref[...] = rhs
    along_ref[...] = jnp.broadcast_to(jnp.sum(rhs * rhs), along_ref.shape)
    spectrum_to(spec_ref, rhs, high_ref, low_ref)


def middle_kernel(
    back_ref, rhs_ref, momentum_ref, high_ref, low_ref, residual_ref, spec_ref, along_ref, step_ref
):
    step = step_of(back_ref)
    step_ref[...] = jnp.broadcast_to(step, step_ref.shape)
    image = taps_of(back_ref, high_ref, low_ref, residual_ref.shape[0])
    rhs = rhs_ref[...]
    residual = rhs - step * image
    direction = residual + momentum_ref[0:1, 0:1] * rhs
    residual_ref[...] = residual
    along_ref[...] = jnp.broadcast_to(jnp.sum(residual * direction), along_ref.shape)
    spectrum_to(spec_ref, direction, high_ref, low_ref)


def last_kernel(
    back_ref, rhs_ref, residual_ref, step_ref, momentum_ref, high_ref, low_ref,
    filters_out, residual_out,
):
    step = step_of(back_ref)
    rhs = rhs_ref[...]
    residual = residual_ref[...]
    direction = residual + momentum_ref[0:1, 0:1] * rhs
    filters_out[...] = step_ref[0:1, 0:1] * rhs + step * direction
    image = taps_of(back_ref, high_ref, low_ref, residual_ref.shape[0])
    residual_out[...] = residual - step * image


def vmem():
    return pl.BlockSpec(memory_space=pltpu.VMEM)


def smem():
    return pl.BlockSpec(memory_space=pltpu.SMEM)


def hbm():
    return pl.BlockSpec(memory_space=pltpu.HBM)


def kernel_body(transfer, target, zone_mask, dark_weight, reg_weight, momentum):
    bins, _, mics, speakers = transfer.shape
    targets = target.shape[2]
    devices = F // bins
    rows = targets * (speakers // devices)
    block = pltpu.VMEM((devices, rows, 2 * bins), BF16)
    summed = pltpu.VMEM((devices, rows + 8, 2 * bins), BF16)
    tile = jax.ShapeDtypeStruct((8, 128), F32)
    taps = jax.ShapeDtypeStruct((rows, K), F32)
    gains = jnp.where(zone_mask == 1, jnp.float32(1.0), dark_weight[:, None])
    bright = (zone_mask == 1).astype(F32)
    factors = pltpu.with_memory_space_constraint(table_factors(devices, F, K), pltpu.HBM)
    target = pltpu.with_memory_space_constraint(target, pltpu.HBM)
    momentum = jnp.broadcast_to(momentum, (8, 128))
    weights = pltpu.VMEM((SLOTS, GROUP) + transfer.shape[1:], BF16)
    turning = pltpu.VMEM((speakers // LANES * targets * (2 * bins + PAD), LANES), F32)
    sems = pltpu.SemaphoreType.DMA((2, SLOTS))

    def exchange(payload):
        received = lax.all_to_all(payload, AXES, split_axis=0, concat_axis=0, tiled=True)
        return pltpu.with_memory_space_constraint(received, pltpu.VMEM)

    def call(kernel, name, in_specs, out_shape, scratch=()):
        return pl.pallas_call(
            kernel,
            in_specs=in_specs,
            out_specs=jax.tree.map(lambda _: vmem(), out_shape),
            out_shape=out_shape,
            scratch_shapes=scratch,
            compiler_params=pltpu.CompilerParams(vmem_limit_bytes=VMEM_BYTES),
            name=name,
        )

    normal = call(
        normal_kernel, "normal", [vmem(), vmem(), smem(), vmem(), hbm()],
        summed, [weights, turning, turning, sems],
    )
    table = pltpu.VMEM((2 * F, K), BF16)
    wanted = pltpu.VMEM((SLOTS, GROUP) + target.shape[1:], BF16)
    back, high, low = call(
        rhs_kernel, "rhs_back", [vmem()] * 4 + [hbm(), hbm()], [block, table, table],
        [weights, wanted, turning, sems],
    )(bright, gains, momentum, factors, transfer, target)
    high = pltpu.with_memory_space_constraint(high, pltpu.VMEM)
    low = pltpu.with_memory_space_constraint(low, pltpu.VMEM)
    rhs, spec, along = call(first_kernel, "first_taps", [vmem()] * 3, [taps, block, tile])(
        exchange(back), high, low
    )
    back = normal(exchange(spec), gains, reg_weight, along, transfer)
    residual, spec, along, step = call(
        middle_kernel, "middle_taps", [vmem()] * 5, [taps, block, tile, tile],
    )(exchange(back), rhs, momentum, high, low)
    back = normal(exchange(spec), gains, reg_weight, along, transfer)
    filters, residual = call(
        last_kernel, "last_taps", [vmem()] * 7, [taps, taps]
    )(exchange(back), rhs, residual, step, momentum, high, low)
    shape = (targets, speakers // devices, K)
    return filters.reshape(shape), residual.reshape(shape)


def body(transfer, target, *rest):
    bins, _, mics, speakers = transfer.shape
    devices = F // bins
    whole_tiles = (
        bins == 64
        and speakers == 8 * devices
        and speakers % 128 == 0
        and mics % 128 == 0
        and target.shape[2] == 32
        and devices % 4 == 0
    )
    return (kernel_body if whole_tiles else plain_body)(transfer, target, *rest)


def solution(mesh):
    in_specs = (
        P(AXES, None, None, None),
        P(AXES, None, None, None),
        P(),
        P(),
        P(AXES),
        P(),
    )
    out_specs = (P(None, AXES, None), P(None, AXES, None))
    return jax.shard_map(body, mesh=mesh, in_specs=in_specs, out_specs=out_specs, check_vma=False)
```
